1024 devices in a mesh: space: 64 (over y, x), lane: 16 (over z, core).
Axes of the slice: x: 8, y: 8, z: 8, core: 2. Of those that a mesh axis runs over, the one named last changes fastest.
Arguments:
- positions: float32 [2048, 3, 544], P('space'), may hold values from -6 to 6
- bend_op: float32 [544, 544], replicated, may hold values from -0.25 to 0.25
- send_list: int32 [64, 64], P('space'), may hold values from 0 to 31
- task_target: int32 [1024, 12], P(('space', 'lane')), may hold values from 0 to 31, as said below
- task_source: int32 [1024, 12], P(('space', 'lane')), may hold values from 0 to 95, as said below
- task_count: int32 [1024], P(('space', 'lane')), may hold values from 4 to 12, as said below
Outputs:
- moved_positions: float32 [2048, 3, 544], P(('space', 'lane'))
- velocity: float32 [2048, 3, 544], P(('space', 'lane'))
The draws below stay inside these ranges and needn't reach their ends.
Inputs may be any that keep to these rules, and one draw needn't show every extreme that they name: `task_target`: slots at or beyond the list's task_count hold 0. `task_source`: slots at or beyond the list's task_count hold 0. Every received cell of an owner is the source of at least one live slot of that owner. `task_count`: in each owner exactly one lane has 12 live slots; every other lane has at most 7.
All inputs are finite; a program needn't handle non-finite values.
Results may differ from the reference program's by a relative error of at most 0.00015.
Values sent between devices are 32-bit elements; how exact they have to be, the bound alone decides.
A program may use at most 32 MiB of HBM per device.

```python
import jax
import jax.numpy as jnp
from jax import lax

P_SIZE = 544
CD = 32
G = 1
TASK_CAP = 12
ITERS = 2
OWNERS = 64
CELLS = 2048
GHOSTS = 64
LANE_ROWS = 1024


def task_tables(key):
    base = jax.random.fold_in(key, 4242)
    key_count, key_busy, key_order, key_fill, key_target = jax.random.split(base, 5)
    lane_count = LANE_ROWS // OWNERS
    counts = jax.random.randint(key_count, (OWNERS, lane_count), 4, 8)
    busiest = jax.random.randint(key_busy, (OWNERS, 1), 0, lane_count)
    counts = jnp.where(jnp.arange(lane_count)[None, :] == busiest, TASK_CAP, counts).astype(jnp.int32)
    starts = jnp.cumsum(counts, axis=1) - counts
    slots = jnp.arange(TASK_CAP)[None, None, :]
    ranks = starts[:, :, None] + slots
    live_slots = slots < counts[:, :, None]
    scores = jax.random.randint(key_order, (OWNERS, GHOSTS), 0, 1 << 20) * GHOSTS + jnp.arange(GHOSTS)[None, :]
    ghost_order = jnp.argsort(scores, axis=1)
    picked = jnp.take_along_axis(ghost_order, jnp.minimum(ranks, GHOSTS - 1).reshape(OWNERS, -1), axis=1)
    picked = picked.reshape(ranks.shape)
    filler = jax.random.randint(key_fill, ranks.shape, 0, CD + GHOSTS)
    sources = jnp.where(ranks < GHOSTS, CD + picked, filler)
    sources = jnp.where(live_slots, sources, 0)
    targets = jax.random.randint(key_target, ranks.shape, 0, CD)
    targets = jnp.where(live_slots, targets, 0)
    return (targets.reshape(LANE_ROWS, TASK_CAP).astype(jnp.int32), sources.reshape(LANE_ROWS, TASK_CAP).astype(jnp.int32), counts.reshape(LANE_ROWS).astype(jnp.int32))


def draw_task_target(key, part):
    return task_tables(key)[0]


def draw_task_source(key, part):
    return task_tables(key)[1]


def draw_task_count(key, part):
    return task_tables(key)[2]


def plant(array, own_key, smallest, high):
    longest = array.shape.index(max(array.shape))
    spots = []
    for shift in (0, 1):
        where = [jax.random.randint(jax.random.fold_in(own_key, axis), (), 0, length) for axis, length in enumerate(array.shape)]
        where[longest] = (where[longest] + shift) % array.shape[longest]
        spots.append(tuple(where))
    return array.at[spots[0]].set(smallest).at[spots[1]].set(high)


def shard_levels(key, dims, cuts, smallest, high):
    def one(axis_at, shards_of):
        heights = jax.random.uniform(jax.random.fold_in(jax.random.fold_in(key, 6), axis_at), (shards_of,), jnp.float32, smallest / len(cuts), high / len(cuts))
        return jnp.repeat(jnp.exp(heights), dims[axis_at] // shards_of).reshape((-1,) + (1,) * (len(dims) - axis_at - 1))

    loudness = one(*cuts[0])
    for cut in cuts[1:]:
        loudness = loudness * one(*cut)
    return loudness


def centred(rng, extent, width, limit, cuts=(), kind=jnp.bfloat16):
    array = width * jax.random.normal(rng, extent, jnp.float32)
    if cuts:
        array = array * shard_levels(rng, extent, cuts, -0.22, 0.18)
    return jnp.clip(array, -limit, limit).astype(kind)


def setup_inputs(seed: int = 0) -> dict:
    seeds = jax.random.split(jax.random.key(seed), 7)
    positions = centred(seeds[0], (CELLS, 3, P_SIZE), 1.0, 6.0, ((0, 64),), jnp.float32)
    bend_op = centred(seeds[1], (P_SIZE, P_SIZE), P_SIZE ** -0.5, 0.25, (), jnp.float32)
    send_list = plant(jax.random.randint(seeds[2], (OWNERS, GHOSTS), 0, CD), jax.random.fold_in(seeds[2], 1), 0, CD - 1).astype(jnp.int32)
    task_target = draw_task_target(jax.random.fold_in(seeds[6], 71), 0)
    task_source = draw_task_source(jax.random.fold_in(seeds[6], 71), 0)
    task_count = draw_task_count(jax.random.fold_in(seeds[6], 71), 0)
    return dict(positions=positions, bend_op=bend_op, send_list=send_list, task_target=task_target, task_source=task_source, task_count=task_count)


REGULARIZE = 0.25
TIME_STEP = 0.5

def stokes_tile(target_pos, source_pos, source_force):
    offsets = target_pos[:, :, None] - source_pos[:, None, :]
    distance_sq = lax.optimization_barrier(jnp.sum(offsets * offsets, axis=0))
    inverse = lax.rsqrt(distance_sq + REGULARIZE)
    inverse_cube = inverse * inverse * inverse
    projected = lax.optimization_barrier(jnp.sum(offsets * source_force[:, None, :], axis=0))
    direct = lax.optimization_barrier(jnp.sum(((distance_sq + 2.0 * REGULARIZE) * inverse_cube)[None] * source_force[:, None, :], axis=2))
    tensor_part = lax.optimization_barrier(jnp.sum((projected * inverse_cube)[None] * offsets, axis=2))
    return (direct + tensor_part) / source_pos.shape[1]

def reference(positions, bend_op, send_list, task_target, task_source, task_count):
    owners = send_list.shape[0]
    cells_owner = positions.shape[0] // owners
    lane_count = task_count.shape[0] // owners
    points = positions.shape[2]
    targets = task_target.reshape(owners, lane_count, -1)
    sources = task_source.reshape(owners, lane_count, -1)
    counts = task_count.reshape(owners, lane_count)
    ghost_local = jnp.transpose(send_list.reshape(owners, owners, G), (1, 0, 2)).reshape(owners, owners * G)
    ghost_owner = jnp.repeat(jnp.arange(owners, dtype=jnp.int32), G)
    ghost_global = (ghost_owner[None, :] * cells_owner + ghost_local).astype(jnp.int32)
    current = positions
    velocity = jnp.zeros_like(positions)
    for iteration in range(ITERS):
        forces = jnp.dot(current.reshape(-1, points), bend_op, precision=lax.Precision.HIGHEST, preferred_element_type=jnp.float32).reshape(current.shape)
        own_pos = current.reshape(owners, cells_owner, 3, points)
        own_frc = forces.reshape(owners, cells_owner, 3, points)
        pool_pos = jnp.concatenate([own_pos, current[ghost_global]], axis=1)
        pool_frc = jnp.concatenate([own_frc, forces[ghost_global]], axis=1)

        def owner_speeds(bundle):
            owner_pos, owner_frc, owner_tgt, owner_src, owner_cnt = bundle

            def lane_pass(lane, speeds):

                def task_pass(task, inner):
                    target_row = owner_tgt[lane, task]
                    source_row = owner_src[lane, task]
                    tile_sum = stokes_tile(owner_pos[target_row], owner_pos[source_row], owner_frc[source_row])
                    return inner.at[target_row].add(tile_sum)
                return lax.fori_loop(0, owner_cnt[lane], task_pass, speeds)
            start = jnp.zeros((cells_owner, 3, points), dtype=jnp.float32)
            return lax.fori_loop(0, lane_count, lane_pass, start)
        velocity = lax.map(owner_speeds, (pool_pos, pool_frc, targets, sources, counts)).reshape(current.shape)
        current = current + TIME_STEP * velocity
    return (current, velocity)
```

```python
import functools
import math

import jax
import jax.numpy as jnp
from jax import lax
from jax.experimental import pallas as pl
from jax.experimental.pallas import tpu as pltpu
from jax.sharding import PartitionSpec as P

ITERS = 2
MESH = pl.DeviceIdType.MESH
ROW = 128


def ring_offsets(side):
    def hops(d):
        return min(d, side - d)

    every = [(dy, dx) for dy in range(side) for dx in range(side)]
    return sorted(every, key=lambda o: (hops(o[0]) + hops(o[1]), o))


def split_bf16(value):
    high = value.astype(jnp.bfloat16)
    return high, (value - high.astype(jnp.float32)).astype(jnp.bfloat16)


def kernel(
    cfg,
    own_ref,
    bend_ref,
    send_ref,
    target_ref,
    source_ref,
    count_ref,
    moved_ref,
    vel_ref,
    pool,
    force,
    bend_hi,
    bend_lo,
    out_box,
    ghost_box,
    broad,
    result,
    own_slice,
    move_out,
    move_in,
    last_out,
    last_in,
    task_out,
    task_in,
    picks_v,
    picks_s,
    send_a,
    recv_a,
    relay_a,
    send_c,
    recv_c,
    relay_c,
    send_d,
    recv_d,
    send_t,
    recv_t,
    local_sem,
):
    owners, lanes, cells, points, cap, slots = cfg
    side = math.isqrt(owners)
    half = owners // 2
    planes = lanes // 2
    pool_cells = cells + owners
    width = own_ref.shape[1]
    chunks = width // ROW
    piece = points // lanes
    rows_piece = -(-piece // 8) * 8
    groups = rows_piece // 8
    cell_rows = 3 * rows_piece
    share = cells // lanes
    box_rows = -(-3 * chunks // 8) * 8
    f32 = jnp.float32

    space = lax.axis_index("space")
    lane = lax.axis_index("lane")
    core = lax.rem(lane, 2)
    plane = lane // 2
    partner = lane + 1 - 2 * core
    y, x = space // side, lax.rem(space, side)
    offsets = ring_offsets(side)

    def owner_at(j, which, sign):
        (ay, ax), (by, bx) = offsets[2 * j], offsets[2 * j + 1]
        dy = jnp.where(which == 0, ay, by)
        dx = jnp.where(which == 0, ax, bx)
        ny = lax.rem(y + sign * dy + side, side)
        nx = lax.rem(x + sign * dx + side, side)
        return ny * side + nx

    def unless_self(j, which, act):
        if j == 0:
            pl.when(which == 1)(act)
        else:
            act()

    barrier = pltpu.get_barrier_semaphore()
    for j in range(half):

        def greet(j=j):
            pl.semaphore_signal(
                barrier, inc=1, device_id=(owner_at(j, core, -1), lane), device_id_type=MESH
            )

        unless_self(j, core, greet)
    for o in range(1, lanes):
        pl.semaphore_signal(
            barrier, inc=1, device_id=(space, lax.rem(lane + o, lanes)), device_id_type=MESH
        )

    task_out[...] = jnp.zeros_like(task_out)
    task_out[0:1, 0:cap] = target_ref[...]
    task_out[1:2, 0:cap] = source_ref[...]
    task_out[2:3, 0:1] = count_ref[...]
    task_in[pl.ds(pl.multiple_of(8 * lane, 8), 8), :] = task_out[...]
    for c in range(3):
        pool[0, c * pool_cells : c * pool_cells + cells, :] = own_ref[c * cells : (c + 1) * cells, :]
    bend_hi[...] = jnp.zeros_like(bend_hi)
    bend_lo[...] = jnp.zeros_like(bend_lo)
    high, low = split_bf16(bend_ref[...])
    bend_hi[0:points, 0:points] = high
    bend_lo[0:points, 0:points] = low
    result[...] = jnp.zeros_like(result)

    def stage_ghosts(step):
        for j in range(half):

            def stage(j=j):
                cell = send_ref[0, owner_at(j, core, 1)]
                for c in range(3):
                    row = pool[step, pl.ds(c * pool_cells + cell, 1), :]
                    for k in range(chunks):
                        at = box_rows * j + c * chunks + k
                        out_box[step, at : at + 1, :] = row[:, k * ROW : (k + 1) * ROW]

            unless_self(j, core, stage)

    def ghost_copy(step, j):
        return pltpu.make_async_remote_copy(
            src_ref=out_box.at[step, pl.ds(box_rows * j, box_rows), :],
            dst_ref=ghost_box.at[step, pl.ds(pl.multiple_of(box_rows * space, 8), box_rows), :],
            send_sem=send_a.at[step, j],
            recv_sem=recv_a.at[step, space],
            device_id=(owner_at(j, core, 1), lane),
            device_id_type=MESH,
        )

    def ghost_pass(step, j, which):
        origin = owner_at(j, which, -1)
        at = pl.ds(pl.multiple_of(box_rows * origin, 8), box_rows)
        return pltpu.make_async_remote_copy(
            src_ref=ghost_box.at[step, at, :],
            dst_ref=ghost_box.at[step, at, :],
            send_sem=relay_a.at[step, j],
            recv_sem=recv_a.at[step, origin],
            device_id=(space, partner),
            device_id_type=MESH,
        )

    def exchange_ghosts(step):
        for j in range(half):
            unless_self(j, core, lambda j=j: ghost_copy(step, j).start())

    def collect_ghosts(step):
        for j in range(half):

            def take(j=j):
                ghost_pass(step, j, core).wait_recv()
                ghost_pass(step, j, core).start()

            unless_self(j, core, take)
        for j in range(half):
            unless_self(j, 1 - core, lambda j=j: ghost_pass(step, j, 1 - core).wait_recv())
        cell = send_ref[0, space]
        for c in range(3):
            row = pool[step, pl.ds(c * pool_cells + cell, 1), :]
            for k in range(chunks):
                at = box_rows * space + c * chunks + k
                ghost_box[step, pl.ds(at, 1), :] = row[:, k * ROW : (k + 1) * ROW]
        for c in range(3):
            for d in range(0, owners, 8):
                rows = min(8, owners - d)
                for k in range(chunks):
                    at = c * pool_cells + cells + d
                    pool[step, at : at + rows, k * ROW : (k + 1) * ROW] = ghost_box[
                        step, pl.ds(box_rows * d + c * chunks + k, rows, stride=box_rows), :
                    ]

    def drain_ghosts(step):
        for j in range(half):

            def drain(j=j):
                ghost_copy(step, j).wait_send()
                ghost_pass(step, j, core).wait_send()

            unless_self(j, core, drain)

    def bend(step, first, count):
        for c in range(3):
            at = pl.ds(c * pool_cells + first, count)
            high, low = split_bf16(pool[step, at, :])
            total = jnp.dot(high, bend_hi[...], preferred_element_type=f32)
            total += jnp.dot(low, bend_hi[...], preferred_element_type=f32)
            total += jnp.dot(high, bend_lo[...], preferred_element_type=f32)
            force[at, :] = total

    def spread_targets():
        block = own_slice[...]
        turned = jnp.concatenate(
            [block, jnp.zeros((ROW - cells, ROW), f32)], axis=0
        ).T
        for t in range(cells):
            broad[t] = jnp.broadcast_to(
                turned[0:cell_rows, t : t + 1], (cell_rows, ROW)
            )

    lane_at = lax.broadcasted_iota(jnp.int32, (8, ROW), 1)

    def one_slot(step, slot):
        target = picks_s[0, slot]
        source = picks_s[1, slot]
        there = [
            jnp.broadcast_to(pool[step, pl.ds(c * pool_cells + source, 1), :], (8, width))
            for c in range(3)
        ]
        push = [
            jnp.broadcast_to(force[pl.ds(c * pool_cells + source, 1), :], (8, width))
            for c in range(3)
        ]
        for g in range(groups):
            here = [
                broad[target, c * rows_piece + 8 * g : c * rows_piece + 8 * g + 8, :]
                for c in range(3)
            ]
            off = [
                jnp.concatenate([h] * chunks, axis=1) - p for h, p in zip(here, there)
            ]
            inverse = lax.rsqrt(off[0] * off[0] + off[1] * off[1] + (off[2] * off[2] + 1.0))
            cube = inverse * inverse * inverse
            along = off[0] * push[0] + off[1] * push[1] + off[2] * push[2]
            direct = inverse + cube
            tensor = along * cube
            for c in range(3):
                total = jnp.sum(direct * push[c] + tensor * off[c], axis=1, keepdims=True)
                at = c * rows_piece + 8 * g
                result[at : at + 8, :] = jnp.where(lane_at == slot, total, result[at : at + 8, :])

    def run_tasks(step):
        unroll = next(u for u in (3, 2, 1) if slots % u == 0)

        @pl.loop(0, slots // unroll)
        def _(n):
            for u in range(unroll):
                one_slot(step, n * unroll + u)

    def read_tasks():
        targets = task_in[pl.ds(0, lanes, stride=8), :]
        sources = task_in[pl.ds(1, lanes, stride=8), :]
        counts = jnp.broadcast_to(task_in[pl.ds(2, lanes, stride=8), 0:1], (lanes, ROW))
        row_at = lax.broadcasted_iota(jnp.int32, (lanes, ROW), 0)
        start = jnp.zeros((lanes, ROW), jnp.int32)
        for n in range(lanes - 1):
            start += jnp.where(row_at > n, counts[n : n + 1, :], 0)
        number = lax.broadcasted_iota(jnp.int32, (lanes, ROW), 1) - start
        target = jnp.zeros((lanes, ROW), jnp.int32)
        source = jnp.zeros((lanes, ROW), jnp.int32)
        for j in range(cap):
            hit = (number == j) & (counts > j)
            target += jnp.where(hit, targets[:, j : j + 1], 0)
            source += jnp.where(hit, sources[:, j : j + 1], 0)
        live = (lax.broadcasted_iota(jnp.int32, (1, ROW), 1) < jnp.sum(counts, axis=0, keepdims=True))
        target = jnp.sum(target, axis=0, keepdims=True)
        source = jnp.sum(source, axis=0, keepdims=True)
        picks_v[...] = jnp.zeros_like(picks_v)
        picks_v[0:1, :] = target
        picks_v[1:2, :] = source
        picks_v[2:3, :] = live.astype(jnp.int32)
        copy = pltpu.make_async_copy(picks_v, picks_s, local_sem)
        copy.start()
        copy.wait()

    def velocities():
        match = (
            (lax.broadcasted_iota(jnp.int32, (cells, ROW), 0) == picks_v[0:1, :])
            & (picks_v[2:3, :] > 0)
        ).astype(f32)
        total = lax.dot_general(
            match,
            result[...],
            (((1,), (1,)), ((), ())),
            precision=lax.Precision.HIGHEST,
            preferred_element_type=f32,
        )
        return total * (1.0 / points)

    def assemble(blocks, rows):
        at = lax.broadcasted_iota(jnp.int32, (rows, ROW), 1)
        whole = [[jnp.zeros((rows, ROW), f32) for _ in range(chunks)] for _ in range(3)]
        for n in range(lanes):
            for c in range(3):
                first = piece * n
                shift = (first - c * rows_piece) % ROW
                block = blocks[n] if shift == 0 else pltpu.roll(blocks[n], shift, 1)
                k, low = divmod(first, ROW)
                high = low + piece
                whole[c][k] = jnp.where((at >= low) & (at < high), block, whole[c][k])
                if high > ROW:
                    whole[c][k + 1] = jnp.where(at < high - ROW, block, whole[c][k + 1])
        return whole

    def lane_copies(source_at, inbox, rows, send, recv):
        made = []
        for o in range(1, lanes):
            other = lax.rem(lane + o, lanes)
            made.append(
                pltpu.make_async_remote_copy(
                    src_ref=source_at(other),
                    dst_ref=inbox.at[pl.ds(pl.multiple_of(rows * lane, 8), rows), :],
                    send_sem=send.at[o],
                    recv_sem=recv.at[o],
                    device_id=(space, other),
                    device_id_type=MESH,
                )
            )
        return made

    lane_of = lax.broadcasted_iota(jnp.int32, (width, ROW), 1)
    point_of = lax.broadcasted_iota(jnp.int32, (width, ROW), 0) - piece * lane
    mine = jnp.zeros((cells, ROW), f32)
    for c in range(3):
        pick = (point_of == lane_of - c * rows_piece) & (point_of >= 0) & (point_of < piece)
        mine += jnp.dot(
            pool[0, c * pool_cells : c * pool_cells + cells, :],
            pick.astype(f32),
            precision=lax.Precision.HIGHEST,
            preferred_element_type=f32,
        )
    own_slice[...] = mine
    spread_targets()
    stage_ghosts(0)

    for core_is in range(2):
        pl.when(core == core_is)(
            lambda n=half - 1 + core_is + lanes - 1: pl.semaphore_wait(barrier, n)
        )

    task_copies = lane_copies(lambda other: task_out, task_in, 8, send_t, recv_t)
    for copy in task_copies:
        copy.start()
    exchange_ghosts(0)
    bend(0, 0, cells)
    for copy in task_copies:
        copy.wait()
    read_tasks()
    collect_ghosts(0)
    bend(0, cells, owners)
    run_tasks(0)
    drain_ghosts(0)

    own_slice[...] += velocities()
    move_out[...] = own_slice[...]

    def move_copy(o):
        return pltpu.make_async_remote_copy(
            src_ref=move_out,
            dst_ref=move_in.at[pl.ds(pl.multiple_of(cells * lane, 8), cells), :],
            send_sem=send_c.at[o],
            recv_sem=recv_c.at[lane],
            device_id=(space, 2 * lax.rem(plane + o, planes) + core),
            device_id_type=MESH,
        )

    def move_pass(o, which):
        origin = 2 * lax.rem(plane + planes - o, planes) + which
        at = pl.ds(pl.multiple_of(cells * origin, 8), cells)
        return pltpu.make_async_remote_copy(
            src_ref=move_out if o == 0 else move_in.at[at, :],
            dst_ref=move_in.at[at, :],
            send_sem=relay_c.at[o],
            recv_sem=recv_c.at[origin],
            device_id=(space, partner),
            device_id_type=MESH,
        )

    near_first = sorted(range(1, planes), key=lambda o: min(o, planes - o))
    for o in near_first:
        move_copy(o).start()
    move_pass(0, core).start()
    move_in[pl.ds(pl.multiple_of(cells * lane, 8), cells), :] = own_slice[...]
    spread_targets()
    for o in near_first:
        move_pass(o, core).wait_recv()
        move_pass(o, core).start()
    for o in range(planes):
        move_pass(o, 1 - core).wait_recv()
    whole = assemble([move_in[cells * n : cells * (n + 1), :] for n in range(lanes)], cells)
    for c in range(3):
        for k in range(chunks):
            at = c * pool_cells
            pool[1, at : at + cells, k * ROW : (k + 1) * ROW] = whole[c][k]

    stage_ghosts(1)
    exchange_ghosts(1)
    bend(1, 0, cells)
    for o in near_first:
        move_copy(o).wait_send()
    for o in range(planes):
        move_pass(o, core).wait_send()
    collect_ghosts(1)
    bend(1, cells, owners)
    run_tasks(1)
    drain_ghosts(1)

    speed = velocities()
    last_out[...] = jnp.zeros_like(last_out)
    for n in range(lanes):
        last_out[8 * n : 8 * n + share, :] = speed[n * share : (n + 1) * share, :]
    last_copies = lane_copies(
        lambda other: last_out.at[pl.ds(pl.multiple_of(8 * other, 8), 8), :],
        last_in,
        8,
        send_d,
        recv_d,
    )
    for copy in last_copies:
        copy.start()
    here = pl.ds(pl.multiple_of(8 * lane, 8), 8)
    last_in[here, :] = last_out[here, :]
    for copy in last_copies:
        copy.wait()
    whole = assemble([last_in[8 * n : 8 * (n + 1), :] for n in range(lanes)], 8)
    for c in range(3):
        speeds = jnp.concatenate(whole[c], axis=1)
        for n in range(share):
            cell = pool[1, pl.ds(c * pool_cells + share * lane + n, 1), :]
            vel_ref[n, c : c + 1, :] = speeds[n : n + 1, 0:points]
            moved_ref[n, c : c + 1, :] = (0.5 * (cell + speeds[n : n + 1, :]))[:, 0:points]


def shards(owners, lanes, positions, bend_op, send_list, task_target, task_source, task_count):
    cells, _, points = positions.shape
    cap = task_target.shape[1]
    slots = cap + 7 * (lanes - 1)
    width = -(-points // ROW) * ROW
    chunks = width // ROW
    piece = points // lanes
    rows_piece = -(-piece // 8) * 8
    cell_rows = 3 * rows_piece
    box_rows = -(-3 * chunks // 8) * 8
    share = cells // lanes
    pool_cells = cells + owners
    half = owners // 2
    planes = lanes // 2
    f32 = jnp.float32
    own = jnp.pad(
        2.0 * jnp.transpose(positions, (1, 0, 2)), ((0, 0), (0, 0), (0, width - points))
    ).reshape(3 * cells, width)
    vmem = pl.BlockSpec(memory_space=pltpu.VMEM)
    smem = pl.BlockSpec(memory_space=pltpu.SMEM)
    dma = pltpu.SemaphoreType.DMA
    out = jax.ShapeDtypeStruct((share, 3, points), f32)
    return pl.pallas_call(
        functools.partial(kernel, (owners, lanes, cells, points, cap, slots)),
        out_shape=(out, out),
        in_specs=[vmem, vmem, smem, vmem, vmem, vmem],
        out_specs=(vmem, vmem),
        scratch_shapes=[
            pltpu.VMEM((ITERS, 3 * pool_cells, width), f32),
            pltpu.VMEM((3 * pool_cells, width), f32),
            pltpu.VMEM((width, width), jnp.bfloat16),
            pltpu.VMEM((width, width), jnp.bfloat16),
            pltpu.VMEM((ITERS, half * box_rows, ROW), f32),
            pltpu.VMEM((ITERS, owners * box_rows, ROW), f32),
            pltpu.VMEM((cells, cell_rows, ROW), f32),
            pltpu.VMEM((ROW, ROW), f32),
            pltpu.VMEM((cells, ROW), f32),
            pltpu.VMEM((cells, ROW), f32),
            pltpu.VMEM((lanes * cells, ROW), f32),
            pltpu.VMEM((lanes * 8, ROW), f32),
            pltpu.VMEM((lanes * 8, ROW), f32),
            pltpu.VMEM((8, ROW), jnp.int32),
            pltpu.VMEM((lanes * 8, ROW), jnp.int32),
            pltpu.VMEM((8, ROW), jnp.int32),
            pltpu.SMEM((8, ROW), jnp.int32),
            dma((ITERS, half)),
            dma((ITERS, owners)),
            dma((ITERS, half)),
            dma((planes,)),
            dma((lanes,)),
            dma((planes,)),
            dma((lanes,)),
            dma((lanes,)),
            dma((lanes,)),
            dma((lanes,)),
            dma,
        ],
        compiler_params=pltpu.CompilerParams(
            collective_id=0, has_side_effects=True, vmem_limit_bytes=48 * 1024 * 1024
        ),
    )(own, bend_op, send_list, task_target, task_source, task_count.reshape(1, 1))


def solution(mesh):
    owners, lanes = mesh.shape["space"], mesh.shape["lane"]
    in_specs = (
        P("space", None, None),
        P(),
        P("space", None),
        P(("space", "lane"), None),
        P(("space", "lane"), None),
        P(("space", "lane")),
    )
    out_specs = (P(("space", "lane"), None, None), P(("space", "lane"), None, None))
    return jax.shard_map(
        functools.partial(shards, owners, lanes),
        mesh=mesh,
        in_specs=in_specs,
        out_specs=out_specs,
        check_vma=False,
    )
```

```python
import functools
import math

import jax
import jax.numpy as jnp
from jax import lax
from jax.experimental import pallas as pl
from jax.experimental.pallas import tpu as pltpu
from jax.sharding import PartitionSpec as P

ITERS = 2
MESH = pl.DeviceIdType.MESH
ROW = 128
SEGMENT = 32


def ring_offsets(side):
    def hops(d):
        return min(d, side - d)

    every = [(dy, dx) for dy in range(side) for dx in range(side)]
    return sorted(every, key=lambda o: (hops(o[0]) + hops(o[1]), o))


def split_bf16(value):
    high = value.astype(jnp.bfloat16)
    return high, (value - high.astype(jnp.float32)).astype(jnp.bfloat16)


def kernel(
    cfg,
    own_hbm,
    bend_hbm,
    send_hbm,
    target_hbm,
    source_hbm,
    count_hbm,
    moved_ref,
    vel_ref,
    pool,
    force,
    bend_hi,
    bend_lo,
    out_box,
    ghost_box,
    broad,
    result,
    own_slice,
    move_out,
    move_in,
    last_out,
    last_in,
    task_out,
    task_in,
    picks_v,
    picks_s,
    send_a,
    recv_a,
    relay_a,
    send_c,
    recv_c,
    relay_c,
    send_d,
    recv_d,
    send_t,
    recv_t,
    local_sem,
    own_ref,
    bend_ref,
    send_ref,
    target_ref,
    source_ref,
    count_ref,
    load_sem,
    result_tail,
):
    owners, lanes, cells, points, cap, slots = cfg
    side = math.isqrt(owners)
    half = owners // 2
    planes = lanes // 2
    pool_cells = cells + owners
    width = pool.shape[2]
    chunks = width // ROW
    full = points // ROW
    piece = points // lanes
    rows_piece = -(-piece // 8) * 8
    groups = piece // 8
    assert chunks == full + 1 and points % ROW <= SEGMENT and groups == 4 and piece % 8 == 2
    quads = -(-slots // 4)
    cell_rows = 3 * rows_piece
    share = cells // lanes
    box_rows = -(-3 * chunks // 8) * 8
    f32 = jnp.float32

    space = lax.axis_index("space")
    lane = lax.axis_index("lane")
    core = lax.rem(lane, 2)
    plane = lane // 2
    partner = lane + 1 - 2 * core
    y, x = space // side, lax.rem(space, side)
    offsets = ring_offsets(side)

    def owner_at(j, which, sign):
        (ay, ax), (by, bx) = offsets[2 * j], offsets[2 * j + 1]
        dy = jnp.where(which == 0, ay, by)
        dx = jnp.where(which == 0, ax, bx)
        ny = lax.rem(y + sign * dy + side, side)
        nx = lax.rem(x + sign * dx + side, side)
        return ny * side + nx

    def unless_self(j, which, act):
        if j == 0:
            pl.when(which == 1)(act)
        else:
            act()

    barrier = pltpu.get_barrier_semaphore()
    for j in range(half):

        def greet(j=j):
            pl.semaphore_signal(
                barrier, inc=1, device_id=(owner_at(j, core, -1), lane), device_id_type=MESH
            )

        unless_self(j, core, greet)
    for o in range(1, lanes):
        pl.semaphore_signal(
            barrier, inc=1, device_id=(space, lax.rem(lane + o, lanes)), device_id_type=MESH
        )

    loads = [
        pltpu.make_async_copy(src, dst, load_sem.at[n])
        for n, (src, dst) in enumerate(
            (
                (target_hbm, target_ref),
                (source_hbm, source_ref),
                (count_hbm, count_ref),
                (own_hbm, own_ref),
                (send_hbm, send_ref),
                (bend_hbm, bend_ref),
            )
        )
    ]
    for load in loads:
        load.start()

    def tail(value):
        rest = value[:, full * ROW : points]
        if rest.shape[1] < SEGMENT:
            rest = jnp.concatenate(
                [rest, jnp.zeros((rest.shape[0], SEGMENT - rest.shape[1]), rest.dtype)], axis=1
            )
        return jnp.concatenate([rest] * (ROW // SEGMENT), axis=1)

    result[...] = jnp.zeros_like(result)
    bend_hi[points:, :] = jnp.zeros((width - points, width), jnp.bfloat16)
    bend_lo[points:, :] = jnp.zeros((width - points, width), jnp.bfloat16)
    for load in loads[:3]:
        load.wait()
    task_out[...] = jnp.zeros_like(task_out)
    task_out[0:1, 0:cap] = target_ref[...]
    task_out[1:2, 0:cap] = source_ref[...]
    task_out[2:3, 0:1] = count_ref[...]
    task_in[pl.ds(pl.multiple_of(8 * lane, 8), 8), :] = task_out[...]
    loads[3].wait()
    for c in range(3):
        at = c * pool_cells
        value = 2.0 * own_ref[:, c, :]
        pool[0, at : at + cells, 0 : full * ROW] = value[:, 0 : full * ROW]
        pool[0, at : at + cells, full * ROW :] = tail(value)
    loads[4].wait()

    def stage_ghosts(step):
        for j in range(half):

            def stage(j=j):
                cell = send_ref[0, owner_at(j, core, 1)]
                for c in range(3):
                    row = pool[step, pl.ds(c * pool_cells + cell, 1), :]
                    for k in range(chunks):
                        at = box_rows * j + c * chunks + k
                        out_box[step, at : at + 1, :] = row[:, k * ROW : (k + 1) * ROW]

            unless_self(j, core, stage)

    def ghost_copy(step, j):
        return pltpu.make_async_remote_copy(
            src_ref=out_box.at[step, pl.ds(box_rows * j, box_rows), :],
            dst_ref=ghost_box.at[step, pl.ds(pl.multiple_of(box_rows * space, 8), box_rows), :],
            send_sem=send_a.at[step, j],
            recv_sem=recv_a.at[step, space],
            device_id=(owner_at(j, core, 1), lane),
            device_id_type=MESH,
        )

    def ghost_pass(step, j, which):
        origin = owner_at(j, which, -1)
        at = pl.ds(pl.multiple_of(box_rows * origin, 8), box_rows)
        return pltpu.make_async_remote_copy(
            src_ref=ghost_box.at[step, at, :],
            dst_ref=ghost_box.at[step, at, :],
            send_sem=relay_a.at[step, j],
            recv_sem=recv_a.at[step, origin],
            device_id=(space, partner),
            device_id_type=MESH,
        )

    def exchange_ghosts(step):
        for j in range(half):
            unless_self(j, core, lambda j=j: ghost_copy(step, j).start())

    def collect_ghosts(step):
        for j in range(half):

            def take(j=j):
                ghost_pass(step, j, core).wait_recv()
                ghost_pass(step, j, core).start()

            unless_self(j, core, take)
        for j in range(half):
            unless_self(j, 1 - core, lambda j=j: ghost_pass(step, j, 1 - core).wait_recv())
        cell = send_ref[0, space]
        for c in range(3):
            row = pool[step, pl.ds(c * pool_cells + cell, 1), :]
            for k in range(chunks):
                at = box_rows * space + c * chunks + k
                ghost_box[step, pl.ds(at, 1), :] = row[:, k * ROW : (k + 1) * ROW]
        for c in range(3):
            for d in range(0, owners, 8):
                rows = min(8, owners - d)
                for k in range(chunks):
                    at = c * pool_cells + cells + d
                    pool[step, at : at + rows, k * ROW : (k + 1) * ROW] = ghost_box[
                        step, pl.ds(box_rows * d + c * chunks + k, rows, stride=box_rows), :
                    ]

    def drain_ghosts(step):
        for j in range(half):

            def drain(j=j):
                ghost_copy(step, j).wait_send()
                ghost_pass(step, j, core).wait_send()

            unless_self(j, core, drain)

    def bend(step, first, count):
        for c in range(3):
            at = pl.ds(c * pool_cells + first, count)
            high, low = split_bf16(pool[step, at, :])
            total = jnp.dot(high, bend_hi[...], preferred_element_type=f32)
            total += jnp.dot(low, bend_hi[...], preferred_element_type=f32)
            total += jnp.dot(high, bend_lo[...], preferred_element_type=f32)
            force[at, :] = total

    lane_at = lax.broadcasted_iota(jnp.int32, (8, ROW), 1)
    row_pair = lax.broadcasted_iota(jnp.int32, (8, ROW), 0) // 2

    def spread_targets():
        block = own_slice[...]
        turned = jnp.concatenate(
            [block, jnp.zeros((ROW - cells, ROW), f32)], axis=0
        ).T
        for t in range(cells):
            block = jnp.broadcast_to(turned[0:cell_rows, t : t + 1], (cell_rows, ROW))
            broad[t, 0:cell_rows, :] = block
            for c in range(3):
                mixed = block[c * rows_piece : c * rows_piece + 8]
                for g in range(1, groups):
                    at = c * rows_piece + 8 * g
                    mixed = jnp.where(lane_at >= SEGMENT * g, block[at : at + 8], mixed)
                broad[t, cell_rows + 8 * c : cell_rows + 8 * c + 8, :] = mixed

    def terms(here, there, push):
        off = [h - p for h, p in zip(here, there)]
        inverse = lax.rsqrt(off[0] * off[0] + off[1] * off[1] + (off[2] * off[2] + 1.0))
        cube = inverse * inverse * inverse
        along = off[0] * push[0] + off[1] * push[1] + off[2] * push[2]
        direct = inverse + cube
        tensor = along * cube
        return [direct * f + tensor * o for f, o in zip(push, off)]

    def wide(block, times):
        return jnp.concatenate([block] * times, axis=1)

    def folded(value):
        total = value[:, 0:ROW]
        for k in range(1, value.shape[1] // ROW):
            total += value[:, k * ROW : (k + 1) * ROW]
        return total

    def place(box, at, lane_here, value):
        total = jnp.sum(value, axis=1, keepdims=True)
        box[at : at + 8, :] = jnp.where(lane_at == lane_here, total, box[at : at + 8, :])

    def four_slots(step, n):
        last_here = last_there = last_push = None
        for j in range(4):
            slot = n + quads * j
            target = picks_s[0, slot]
            source = picks_s[1, slot]
            there = [
                jnp.broadcast_to(pool[step, pl.ds(c * pool_cells + source, 1), :], (8, width))
                for c in range(3)
            ]
            push = [
                jnp.broadcast_to(force[pl.ds(c * pool_cells + source, 1), :], (8, width))
                for c in range(3)
            ]
            mixed = terms(
                [broad[target, cell_rows + 8 * c : cell_rows + 8 * c + 8, :] for c in range(3)],
                [p[:, full * ROW :] for p in there],
                [p[:, full * ROW :] for p in push],
            )
            for g in range(groups):
                rows = [c * rows_piece + 8 * g for c in range(3)]
                here = [wide(broad[target, r : r + 8, :], full) for r in rows]
                whole = terms(
                    here, [p[:, : full * ROW] for p in there], [p[:, : full * ROW] for p in push]
                )
                part = (lane_at >= SEGMENT * g) & (lane_at < SEGMENT * (g + 1))
                for c in range(3):
                    place(result, rows[c], slot, folded(whole[c]) + jnp.where(part, mixed[c], 0.0))
            rows = [c * rows_piece + 8 * groups for c in range(3)]
            here = [broad[target, r : r + 8, :] for r in rows]
            if j == 0:
                last_here, last_there, last_push = here, there, push
            else:
                own = row_pair == j
                own_wide = wide(own, chunks)
                last_here = [jnp.where(own, a, b) for a, b in zip(here, last_here)]
                last_there = [jnp.where(own_wide, a, b) for a, b in zip(there, last_there)]
                last_push = [jnp.where(own_wide, a, b) for a, b in zip(push, last_push)]
        whole = terms([wide(h, chunks) for h in last_here], last_there, last_push)
        for c in range(3):
            value = folded(whole[c][:, : full * ROW]) + jnp.where(
                lane_at < SEGMENT, whole[c][:, full * ROW :], 0.0
            )
            place(result_tail, 8 * c, n, value)

    def run_tasks(step):
        result_tail[...] = jnp.zeros_like(result_tail)

        @pl.loop(0, quads)
        def _(n):
            four_slots(step, n)

        even = lax.broadcasted_iota(jnp.int32, (8, ROW), 0) % 2 == 0
        for c in range(3):
            block = jnp.zeros((8, ROW), f32)
            for j in range(4):
                pair = [
                    result_tail[8 * c + 2 * j + i : 8 * c + 2 * j + i + 1, :] for i in range(2)
                ]
                rows = jnp.where(
                    even,
                    jnp.broadcast_to(pair[0], (8, ROW)),
                    jnp.broadcast_to(pair[1], (8, ROW)),
                )
                if j:
                    rows = pltpu.roll(rows, quads * j, 1)
                mine = (lane_at >= quads * j) & (lane_at < quads * (j + 1))
                block = jnp.where(mine, rows, block)
            at = c * rows_piece + 8 * groups
            result[at : at + 8, :] = block

    def read_tasks():
        targets = task_in[pl.ds(0, lanes, stride=8), :]
        sources = task_in[pl.ds(1, lanes, stride=8), :]
        counts = jnp.broadcast_to(task_in[pl.ds(2, lanes, stride=8), 0:1], (lanes, ROW))
        row_at = lax.broadcasted_iota(jnp.int32, (lanes, ROW), 0)
        start = jnp.zeros((lanes, ROW), jnp.int32)
        for n in range(lanes - 1):
            start += jnp.where(row_at > n, counts[n : n + 1, :], 0)
        number = lax.broadcasted_iota(jnp.int32, (lanes, ROW), 1) - start
        target = jnp.zeros((lanes, ROW), jnp.int32)
        source = jnp.zeros((lanes, ROW), jnp.int32)
        for j in range(cap):
            hit = (number == j) & (counts > j)
            target += jnp.where(hit, targets[:, j : j + 1], 0)
            source += jnp.where(hit, sources[:, j : j + 1], 0)
        live = (lax.broadcasted_iota(jnp.int32, (1, ROW), 1) < jnp.sum(counts, axis=0, keepdims=True))
        target = jnp.sum(target, axis=0, keepdims=True)
        source = jnp.sum(source, axis=0, keepdims=True)
        picks_v[...] = jnp.zeros_like(picks_v)
        picks_v[0:1, :] = target
        picks_v[1:2, :] = source
        picks_v[2:3, :] = live.astype(jnp.int32)
        copy = pltpu.make_async_copy(picks_v, picks_s, local_sem)
        copy.start()
        copy.wait()

    def velocities():
        match = (
            (lax.broadcasted_iota(jnp.int32, (cells, ROW), 0) == picks_v[0:1, :])
            & (picks_v[2:3, :] > 0)
        ).astype(f32)
        total = lax.dot_general(
            match,
            result[...],
            (((1,), (1,)), ((), ())),
            precision=lax.Precision.HIGHEST,
            preferred_element_type=f32,
        )
        return total * (1.0 / points)

    def assemble(blocks, rows):
        at = lax.broadcasted_iota(jnp.int32, (rows, ROW), 1)
        whole = [[jnp.zeros((rows, ROW), f32) for _ in range(chunks)] for _ in range(3)]
        for n in range(lanes):
            for c in range(3):
                first = piece * n
                shift = (first - c * rows_piece) % ROW
                block = blocks[n] if shift == 0 else pltpu.roll(blocks[n], shift, 1)
                k, low = divmod(first, ROW)
                high = low + piece
                whole[c][k] = jnp.where((at >= low) & (at < high), block, whole[c][k])
                if high > ROW:
                    whole[c][k + 1] = jnp.where(at < high - ROW, block, whole[c][k + 1])
        for c in range(3):
            rest = whole[c][full]
            whole[c][full] = sum(
                (pltpu.roll(rest, SEGMENT * q, 1) for q in range(1, ROW // SEGMENT)), rest
            )
        return whole

    def lane_copies(source_at, inbox, rows, send, recv):
        made = []
        for o in range(1, lanes):
            other = lax.rem(lane + o, lanes)
            made.append(
                pltpu.make_async_remote_copy(
                    src_ref=source_at(other),
                    dst_ref=inbox.at[pl.ds(pl.multiple_of(rows * lane, 8), rows), :],
                    send_sem=send.at[o],
                    recv_sem=recv.at[o],
                    device_id=(space, other),
                    device_id_type=MESH,
                )
            )
        return made

    lane_of = lax.broadcasted_iota(jnp.int32, (width, ROW), 1)
    point_of = lax.broadcasted_iota(jnp.int32, (width, ROW), 0) - piece * lane
    mine = jnp.zeros((cells, ROW), f32)
    for c in range(3):
        nth = lane_of - c * rows_piece
        nth = jnp.where(nth < piece, nth, 8 * groups + lax.rem(nth, 2))
        inside = (lane_of >= c * rows_piece) & (lane_of < (c + 1) * rows_piece)
        pick = (point_of == nth) & inside
        mine += jnp.dot(
            pool[0, c * pool_cells : c * pool_cells + cells, :],
            pick.astype(f32),
            precision=lax.Precision.HIGHEST,
            preferred_element_type=f32,
        )
    own_slice[...] = mine
    stage_ghosts(0)
    spread_targets()
    loads[5].wait()
    bend_op = bend_ref[...]
    for at, value in ((0, bend_op[:, 0 : full * ROW]), (full * ROW, tail(bend_op))):
        high, low = split_bf16(value)
        bend_hi[0:points, at : at + value.shape[1]] = high
        bend_lo[0:points, at : at + value.shape[1]] = low

    for core_is in range(2):
        pl.when(core == core_is)(
            lambda n=half - 1 + core_is + lanes - 1: pl.semaphore_wait(barrier, n)
        )

    task_copies = lane_copies(lambda other: task_out, task_in, 8, send_t, recv_t)
    for copy in task_copies:
        copy.start()
    exchange_ghosts(0)
    bend(0, 0, cells)
    for copy in task_copies:
        copy.wait()
    read_tasks()
    collect_ghosts(0)
    bend(0, cells, owners)
    run_tasks(0)
    drain_ghosts(0)

    own_slice[...] += velocities()
    move_out[...] = own_slice[...]

    def move_copy(o):
        return pltpu.make_async_remote_copy(
            src_ref=move_out,
            dst_ref=move_in.at[pl.ds(pl.multiple_of(cells * lane, 8), cells), :],
            send_sem=send_c.at[o],
            recv_sem=recv_c.at[lane],
            device_id=(space, 2 * lax.rem(plane + o, planes) + core),
            device_id_type=MESH,
        )

    def move_pass(o, which):
        origin = 2 * lax.rem(plane + planes - o, planes) + which
        at = pl.ds(pl.multiple_of(cells * origin, 8), cells)
        return pltpu.make_async_remote_copy(
            src_ref=move_out if o == 0 else move_in.at[at, :],
            dst_ref=move_in.at[at, :],
            send_sem=relay_c.at[o],
            recv_sem=recv_c.at[origin],
            device_id=(space, partner),
            device_id_type=MESH,
        )

    near_first = sorted(range(1, planes), key=lambda o: min(o, planes - o))
    for o in near_first:
        move_copy(o).start()
    move_pass(0, core).start()
    move_in[pl.ds(pl.multiple_of(cells * lane, 8), cells), :] = own_slice[...]
    spread_targets()
    for o in near_first:
        move_pass(o, core).wait_recv()
        move_pass(o, core).start()
    for o in range(planes):
        move_pass(o, 1 - core).wait_recv()
    whole = assemble([move_in[cells * n : cells * (n + 1), :] for n in range(lanes)], cells)
    for c in range(3):
        for k in range(chunks):
            at = c * pool_cells
            pool[1, at : at + cells, k * ROW : (k + 1) * ROW] = whole[c][k]

    stage_ghosts(1)
    exchange_ghosts(1)
    bend(1, 0, cells)
    for o in near_first:
        move_copy(o).wait_send()
    for o in range(planes):
        move_pass(o, core).wait_send()
    collect_ghosts(1)
    bend(1, cells, owners)
    run_tasks(1)
    drain_ghosts(1)

    speed = velocities()
    last_out[...] = jnp.zeros_like(last_out)
    for n in range(lanes):
        last_out[8 * n : 8 * n + share, :] = speed[n * share : (n + 1) * share, :]
    last_copies = lane_copies(
        lambda other: last_out.at[pl.ds(pl.multiple_of(8 * other, 8), 8), :],
        last_in,
        8,
        send_d,
        recv_d,
    )
    for copy in last_copies:
        copy.start()
    here = pl.ds(pl.multiple_of(8 * lane, 8), 8)
    last_in[here, :] = last_out[here, :]
    for copy in last_copies:
        copy.wait()
    whole = assemble([last_in[8 * n : 8 * (n + 1), :] for n in range(lanes)], 8)
    for c in range(3):
        speeds = jnp.concatenate(whole[c], axis=1)
        for n in range(share):
            cell = pool[1, pl.ds(c * pool_cells + share * lane + n, 1), :]
            vel_ref[n, c : c + 1, :] = speeds[n : n + 1, 0:points]
            moved_ref[n, c : c + 1, :] = (0.5 * (cell + speeds[n : n + 1, :]))[:, 0:points]


def shards(owners, lanes, positions, bend_op, send_list, task_target, task_source, task_count):
    cells, _, points = positions.shape
    cap = task_target.shape[1]
    slots = cap + 7 * (lanes - 1)
    width = -(-points // ROW) * ROW
    chunks = width // ROW
    piece = points // lanes
    rows_piece = -(-piece // 8) * 8
    cell_rows = 3 * rows_piece
    box_rows = -(-3 * chunks // 8) * 8
    share = cells // lanes
    pool_cells = cells + owners
    half = owners // 2
    planes = lanes // 2
    f32 = jnp.float32
    vmem = pl.BlockSpec(memory_space=pltpu.VMEM)
    hbm = pl.BlockSpec(memory_space=pltpu.HBM)
    dma = pltpu.SemaphoreType.DMA
    out = jax.ShapeDtypeStruct((share, 3, points), f32)
    return pl.pallas_call(
        functools.partial(kernel, (owners, lanes, cells, points, cap, slots)),
        out_shape=(out, out),
        in_specs=[hbm] * 6,
        out_specs=(vmem, vmem),
        scratch_shapes=[
            pltpu.VMEM((ITERS, 3 * pool_cells, width), f32),
            pltpu.VMEM((3 * pool_cells, width), f32),
            pltpu.VMEM((width, width), jnp.bfloat16),
            pltpu.VMEM((width, width), jnp.bfloat16),
            pltpu.VMEM((ITERS, half * box_rows, ROW), f32),
            pltpu.VMEM((ITERS, owners * box_rows, ROW), f32),
            pltpu.VMEM((cells, cell_rows + 24, ROW), f32),
            pltpu.VMEM((ROW, ROW), f32),
            pltpu.VMEM((cells, ROW), f32),
            pltpu.VMEM((cells, ROW), f32),
            pltpu.VMEM((lanes * cells, ROW), f32),
            pltpu.VMEM((lanes * 8, ROW), f32),
            pltpu.VMEM((lanes * 8, ROW), f32),
            pltpu.VMEM((8, ROW), jnp.int32),
            pltpu.VMEM((lanes * 8, ROW), jnp.int32),
            pltpu.VMEM((8, ROW), jnp.int32),
            pltpu.SMEM((8, ROW), jnp.int32),
            dma((ITERS, half)),
            dma((ITERS, owners)),
            dma((ITERS, half)),
            dma((planes,)),
            dma((lanes,)),
            dma((planes,)),
            dma((lanes,)),
            dma((lanes,)),
            dma((lanes,)),
            dma((lanes,)),
            dma,
            pltpu.VMEM(positions.shape, f32),
            pltpu.VMEM(bend_op.shape, f32),
            pltpu.SMEM(send_list.shape, jnp.int32),
            pltpu.VMEM((1, cap), jnp.int32),
            pltpu.VMEM((1, cap), jnp.int32),
            pltpu.VMEM((1, 1), jnp.int32),
            dma((6,)),
            pltpu.VMEM((24, ROW), f32),
        ],
        compiler_params=pltpu.CompilerParams(
            collective_id=0, has_side_effects=True, vmem_limit_bytes=48 * 1024 * 1024
        ),
    )(positions, bend_op, send_list, task_target, task_source, task_count.reshape(1, 1))


def solution(mesh):
    owners, lanes = mesh.shape["space"], mesh.shape["lane"]
    in_specs = (
        P("space", None, None),
        P(),
        P("space", None),
        P(("space", "lane"), None),
        P(("space", "lane"), None),
        P(("space", "lane")),
    )
    out_specs = (P(("space", "lane"), None, None), P(("space", "lane"), None, None))
    return jax.shard_map(
        functools.partial(shards, owners, lanes),
        mesh=mesh,
        in_specs=in_specs,
        out_specs=out_specs,
        check_vma=False,
    )
```

```python
import functools
import math

import jax
import jax.numpy as jnp
from jax import lax
from jax.experimental import pallas as pl
from jax.experimental.pallas import tpu as pltpu
from jax.sharding import PartitionSpec as P

ITERS = 2
MESH = pl.DeviceIdType.MESH
ROW = 128
SEGMENT = 32


def ring_offsets(side):
    def hops(d):
        return min(d, side - d)

    every = [(dy, dx) for dy in range(side) for dx in range(side)]
    return sorted(every, key=lambda o: (hops(o[0]) + hops(o[1]), o))


def split_bf16(value):
    high = value.astype(jnp.bfloat16)
    return high, (value - high.astype(jnp.float32)).astype(jnp.bfloat16)


def kernel(
    cfg,
    own_hbm,
    bend_hbm,
    send_hbm,
    target_hbm,
    source_hbm,
    count_hbm,
    moved_ref,
    vel_ref,
    pool,
    force,
    bend_hi,
    bend_lo,
    out_box,
    ghost_box,
    broad,
    result,
    own_slice,
    move_out,
    move_in,
    last_out,
    last_in,
    task_out,
    task_in,
    picks_v,
    picks_s,
    send_a,
    recv_a,
    relay_a,
    send_c,
    recv_c,
    relay_c,
    send_d,
    recv_d,
    send_t,
    recv_t,
    local_sem,
    own_ref,
    bend_ref,
    send_ref,
    target_ref,
    source_ref,
    count_ref,
    load_sem,
    result_tail,
):
    owners, lanes, cells, points, cap, slots = cfg
    side = math.isqrt(owners)
    half = owners // 2
    planes = lanes // 2
    pool_cells = cells + owners
    width = pool.shape[2]
    chunks = width // ROW
    full = points // ROW
    piece = points // lanes
    rows_piece = -(-piece // 8) * 8
    groups = piece // 8
    assert chunks == full + 1 and points % ROW <= SEGMENT and groups == 4 and piece % 8 == 2
    quads = -(-slots // 4)
    cell_rows = 3 * rows_piece
    share = cells // lanes
    box_rows = -(-3 * chunks // 8) * 8
    f32 = jnp.float32

    space = lax.axis_index("space")
    lane = lax.axis_index("lane")
    core = lax.rem(lane, 2)
    plane = lane // 2
    partner = lane + 1 - 2 * core
    y, x = space // side, lax.rem(space, side)
    offsets = ring_offsets(side)

    def owner_at(j, which, sign):
        (ay, ax), (by, bx) = offsets[2 * j], offsets[2 * j + 1]
        dy = jnp.where(which == 0, ay, by)
        dx = jnp.where(which == 0, ax, bx)
        ny = lax.rem(y + sign * dy + side, side)
        nx = lax.rem(x + sign * dx + side, side)
        return ny * side + nx

    def unless_self(j, which, act):
        if j == 0:
            pl.when(which == 1)(act)
        else:
            act()

    barrier = pltpu.get_barrier_semaphore()
    for j in range(half):

        def greet(j=j):
            pl.semaphore_signal(
                barrier, inc=1, device_id=(owner_at(j, core, -1), lane), device_id_type=MESH
            )

        unless_self(j, core, greet)
    for o in range(1, lanes):
        pl.semaphore_signal(
            barrier, inc=1, device_id=(space, lax.rem(lane + o, lanes)), device_id_type=MESH
        )

    loads = [
        pltpu.make_async_copy(src, dst, load_sem.at[n])
        for n, (src, dst) in enumerate(
            (
                (target_hbm, target_ref),
                (source_hbm, source_ref),
                (count_hbm, count_ref),
                (own_hbm, own_ref),
                (send_hbm, send_ref),
                (bend_hbm, bend_ref),
            )
        )
    ]
    for load in loads:
        load.start()

    def tail(value):
        rest = value[:, full * ROW : points]
        if rest.shape[1] < SEGMENT:
            rest = jnp.concatenate(
                [rest, jnp.zeros((rest.shape[0], SEGMENT - rest.shape[1]), rest.dtype)], axis=1
            )
        return jnp.concatenate([rest] * (ROW // SEGMENT), axis=1)

    result[...] = jnp.zeros_like(result)
    bend_hi[points:, :] = jnp.zeros((width - points, width), jnp.bfloat16)
    bend_lo[points:, :] = jnp.zeros((width - points, width), jnp.bfloat16)
    for load in loads[:3]:
        load.wait()
    task_out[...] = jnp.zeros_like(task_out)
    task_out[0:1, 0:cap] = target_ref[...]
    task_out[1:2, 0:cap] = source_ref[...]
    task_out[2:3, 0:1] = count_ref[...]
    task_in[pl.ds(pl.multiple_of(8 * lane, 8), 8), :] = task_out[...]
    loads[3].wait()
    for c in range(3):
        at = c * pool_cells
        value = 2.0 * own_ref[c]
        pool[0, at : at + cells, 0 : full * ROW] = value[:, 0 : full * ROW]
        pool[0, at : at + cells, full * ROW :] = tail(value)
    loads[4].wait()

    def stage_ghosts(step):
        for j in range(half):

            def stage(j=j):
                cell = send_ref[0, owner_at(j, core, 1)]
                for c in range(3):
                    row = pool[step, pl.ds(c * pool_cells + cell, 1), :]
                    for k in range(chunks):
                        at = box_rows * j + c * chunks + k
                        out_box[step, at : at + 1, :] = row[:, k * ROW : (k + 1) * ROW]

            unless_self(j, core, stage)

    def ghost_copy(step, j):
        return pltpu.make_async_remote_copy(
            src_ref=out_box.at[step, pl.ds(box_rows * j, box_rows), :],
            dst_ref=ghost_box.at[step, pl.ds(pl.multiple_of(box_rows * space, 8), box_rows), :],
            send_sem=send_a.at[step, j],
            recv_sem=recv_a.at[step, space],
            device_id=(owner_at(j, core, 1), lane),
            device_id_type=MESH,
        )

    def ghost_pass(step, j, which):
        origin = owner_at(j, which, -1)
        at = pl.ds(pl.multiple_of(box_rows * origin, 8), box_rows)
        return pltpu.make_async_remote_copy(
            src_ref=ghost_box.at[step, at, :],
            dst_ref=ghost_box.at[step, at, :],
            send_sem=relay_a.at[step, j],
            recv_sem=recv_a.at[step, origin],
            device_id=(space, partner),
            device_id_type=MESH,
        )

    def exchange_ghosts(step):
        for j in range(half):
            unless_self(j, core, lambda j=j: ghost_copy(step, j).start())

    def collect_ghosts(step):
        for j in range(half):

            def take(j=j):
                ghost_pass(step, j, core).wait_recv()
                ghost_pass(step, j, core).start()

            unless_self(j, core, take)
        for j in range(half):
            unless_self(j, 1 - core, lambda j=j: ghost_pass(step, j, 1 - core).wait_recv())
        cell = send_ref[0, space]
        for c in range(3):
            row = pool[step, pl.ds(c * pool_cells + cell, 1), :]
            for k in range(chunks):
                at = box_rows * space + c * chunks + k
                ghost_box[step, pl.ds(at, 1), :] = row[:, k * ROW : (k + 1) * ROW]
        for c in range(3):
            for d in range(0, owners, 8):
                rows = min(8, owners - d)
                for k in range(chunks):
                    at = c * pool_cells + cells + d
                    pool[step, at : at + rows, k * ROW : (k + 1) * ROW] = ghost_box[
                        step, pl.ds(box_rows * d + c * chunks + k, rows, stride=box_rows), :
                    ]

    def drain_ghosts(step):
        for j in range(half):

            def drain(j=j):
                ghost_copy(step, j).wait_send()
                ghost_pass(step, j, core).wait_send()

            unless_self(j, core, drain)

    def bend(step, first, count):
        for c in range(3):
            at = pl.ds(c * pool_cells + first, count)
            high, low = split_bf16(pool[step, at, :])
            total = jnp.dot(high, bend_hi[...], preferred_element_type=f32)
            total += jnp.dot(low, bend_hi[...], preferred_element_type=f32)
            total += jnp.dot(high, bend_lo[...], preferred_element_type=f32)
            force[at, :] = total

    lane_at = lax.broadcasted_iota(jnp.int32, (8, ROW), 1)
    row_pair = lax.broadcasted_iota(jnp.int32, (8, ROW), 0) // 2

    def spread_targets():
        block = own_slice[...]
        turned = jnp.concatenate(
            [block, jnp.zeros((ROW - cells, ROW), f32)], axis=0
        ).T
        for t in range(cells):
            block = jnp.broadcast_to(turned[0:cell_rows, t : t + 1], (cell_rows, ROW))
            broad[t, 0:cell_rows, :] = block
            for c in range(3):
                mixed = block[c * rows_piece : c * rows_piece + 8]
                for g in range(1, groups):
                    at = c * rows_piece + 8 * g
                    mixed = jnp.where(lane_at >= SEGMENT * g, block[at : at + 8], mixed)
                broad[t, cell_rows + 8 * c : cell_rows + 8 * c + 8, :] = mixed

    def terms(here, there, push):
        off = [h - p for h, p in zip(here, there)]
        inverse = lax.rsqrt(off[0] * off[0] + off[1] * off[1] + (off[2] * off[2] + 1.0))
        cube = inverse * inverse * inverse
        along = off[0] * push[0] + off[1] * push[1] + off[2] * push[2]
        direct = inverse + cube
        tensor = along * cube
        return [direct * f + tensor * o for f, o in zip(push, off)]

    def wide(block, times):
        return jnp.concatenate([block] * times, axis=1)

    def folded(value):
        total = value[:, 0:ROW]
        for k in range(1, value.shape[1] // ROW):
            total += value[:, k * ROW : (k + 1) * ROW]
        return total

    def place(box, at, lane_here, value):
        total = jnp.sum(value, axis=1, keepdims=True)
        box[at : at + 8, :] = jnp.where(lane_at == lane_here, total, box[at : at + 8, :])

    def four_slots(step, n):
        last_here = last_there = last_push = None
        for j in range(4):
            slot = n + quads * j
            target = picks_s[0, slot]
            source = picks_s[1, slot]
            there = [
                jnp.broadcast_to(pool[step, pl.ds(c * pool_cells + source, 1), :], (8, width))
                for c in range(3)
            ]
            push = [
                jnp.broadcast_to(force[pl.ds(c * pool_cells + source, 1), :], (8, width))
                for c in range(3)
            ]
            mixed = terms(
                [broad[target, cell_rows + 8 * c : cell_rows + 8 * c + 8, :] for c in range(3)],
                [p[:, full * ROW :] for p in there],
                [p[:, full * ROW :] for p in push],
            )
            for g in range(groups):
                rows = [c * rows_piece + 8 * g for c in range(3)]
                here = [wide(broad[target, r : r + 8, :], full) for r in rows]
                whole = terms(
                    here, [p[:, : full * ROW] for p in there], [p[:, : full * ROW] for p in push]
                )
                part = (lane_at >= SEGMENT * g) & (lane_at < SEGMENT * (g + 1))
                for c in range(3):
                    place(result, rows[c], slot, folded(whole[c]) + jnp.where(part, mixed[c], 0.0))
            rows = [c * rows_piece + 8 * groups for c in range(3)]
            here = [broad[target, r : r + 8, :] for r in rows]
            if j == 0:
                last_here, last_there, last_push = here, there, push
            else:
                own = row_pair == j
                own_wide = wide(own, chunks)
                last_here = [jnp.where(own, a, b) for a, b in zip(here, last_here)]
                last_there = [jnp.where(own_wide, a, b) for a, b in zip(there, last_there)]
                last_push = [jnp.where(own_wide, a, b) for a, b in zip(push, last_push)]
        whole = terms([wide(h, chunks) for h in last_here], last_there, last_push)
        for c in range(3):
            value = folded(whole[c][:, : full * ROW]) + jnp.where(
                lane_at < SEGMENT, whole[c][:, full * ROW :], 0.0
            )
            place(result_tail, 8 * c, n, value)

    def run_tasks(step):
        result_tail[...] = jnp.zeros_like(result_tail)

        @pl.loop(0, quads)
        def _(n):
            four_slots(step, n)

        even = lax.broadcasted_iota(jnp.int32, (8, ROW), 0) % 2 == 0
        for c in range(3):
            block = jnp.zeros((8, ROW), f32)
            for j in range(4):
                pair = [
                    result_tail[8 * c + 2 * j + i : 8 * c + 2 * j + i + 1, :] for i in range(2)
                ]
                rows = jnp.where(
                    even,
                    jnp.broadcast_to(pair[0], (8, ROW)),
                    jnp.broadcast_to(pair[1], (8, ROW)),
                )
                if j:
                    rows = pltpu.roll(rows, quads * j, 1)
                mine = (lane_at >= quads * j) & (lane_at < quads * (j + 1))
                block = jnp.where(mine, rows, block)
            at = c * rows_piece + 8 * groups
            result[at : at + 8, :] = block

    def read_tasks():
        targets = task_in[pl.ds(0, lanes, stride=8), :]
        sources = task_in[pl.ds(1, lanes, stride=8), :]
        counts = jnp.broadcast_to(task_in[pl.ds(2, lanes, stride=8), 0:1], (lanes, ROW))
        row_at = lax.broadcasted_iota(jnp.int32, (lanes, ROW), 0)
        start = jnp.zeros((lanes, ROW), jnp.int32)
        for n in range(lanes - 1):
            start += jnp.where(row_at > n, counts[n : n + 1, :], 0)
        number = lax.broadcasted_iota(jnp.int32, (lanes, ROW), 1) - start
        target = jnp.zeros((lanes, ROW), jnp.int32)
        source = jnp.zeros((lanes, ROW), jnp.int32)
        for j in range(cap):
            hit = (number == j) & (counts > j)
            target += jnp.where(hit, targets[:, j : j + 1], 0)
            source += jnp.where(hit, sources[:, j : j + 1], 0)
        live = (lax.broadcasted_iota(jnp.int32, (1, ROW), 1) < jnp.sum(counts, axis=0, keepdims=True))
        target = jnp.sum(target, axis=0, keepdims=True)
        source = jnp.sum(source, axis=0, keepdims=True)
        picks_v[...] = jnp.zeros_like(picks_v)
        picks_v[0:1, :] = target
        picks_v[1:2, :] = source
        picks_v[2:3, :] = live.astype(jnp.int32)
        copy = pltpu.make_async_copy(picks_v, picks_s, local_sem)
        copy.start()
        copy.wait()

    def velocities():
        match = (
            (lax.broadcasted_iota(jnp.int32, (cells, ROW), 0) == picks_v[0:1, :])
            & (picks_v[2:3, :] > 0)
        ).astype(f32)
        total = lax.dot_general(
            match,
            result[...],
            (((1,), (1,)), ((), ())),
            precision=lax.Precision.HIGHEST,
            preferred_element_type=f32,
        )
        return total * (1.0 / points)

    def assemble(blocks, rows):
        at = lax.broadcasted_iota(jnp.int32, (rows, ROW), 1)
        whole = [[jnp.zeros((rows, ROW), f32) for _ in range(chunks)] for _ in range(3)]
        for n in range(lanes):
            for c in range(3):
                first = piece * n
                shift = (first - c * rows_piece) % ROW
                block = blocks[n] if shift == 0 else pltpu.roll(blocks[n], shift, 1)
                k, low = divmod(first, ROW)
                high = low + piece
                whole[c][k] = jnp.where((at >= low) & (at < high), block, whole[c][k])
                if high > ROW:
                    whole[c][k + 1] = jnp.where(at < high - ROW, block, whole[c][k + 1])
        for c in range(3):
            rest = whole[c][full]
            whole[c][full] = sum(
                (pltpu.roll(rest, SEGMENT * q, 1) for q in range(1, ROW // SEGMENT)), rest
            )
        return whole

    def lane_copies(source_at, inbox, rows, send, recv):
        made = []
        for o in range(1, lanes):
            other = lax.rem(lane + o, lanes)
            made.append(
                pltpu.make_async_remote_copy(
                    src_ref=source_at(other),
                    dst_ref=inbox.at[pl.ds(pl.multiple_of(rows * lane, 8), rows), :],
                    send_sem=send.at[o],
                    recv_sem=recv.at[o],
                    device_id=(space, other),
                    device_id_type=MESH,
                )
            )
        return made

    lane_of = lax.broadcasted_iota(jnp.int32, (width, ROW), 1)
    point_of = lax.broadcasted_iota(jnp.int32, (width, ROW), 0) - piece * lane
    mine = jnp.zeros((cells, ROW), f32)
    for c in range(3):
        nth = lane_of - c * rows_piece
        nth = jnp.where(nth < piece, nth, 8 * groups + lax.rem(nth, 2))
        inside = (lane_of >= c * rows_piece) & (lane_of < (c + 1) * rows_piece)
        pick = (point_of == nth) & inside
        mine += jnp.dot(
            pool[0, c * pool_cells : c * pool_cells + cells, :],
            pick.astype(f32),
            precision=lax.Precision.HIGHEST,
            preferred_element_type=f32,
        )
    own_slice[...] = mine
    stage_ghosts(0)
    spread_targets()
    loads[5].wait()
    bend_op = bend_ref[...]
    for at, value in ((0, bend_op[:, 0 : full * ROW]), (full * ROW, tail(bend_op))):
        high, low = split_bf16(value)
        bend_hi[0:points, at : at + value.shape[1]] = high
        bend_lo[0:points, at : at + value.shape[1]] = low

    for core_is in range(2):
        pl.when(core == core_is)(
            lambda n=half - 1 + core_is + lanes - 1: pl.semaphore_wait(barrier, n)
        )

    task_copies = lane_copies(lambda other: task_out, task_in, 8, send_t, recv_t)
    for copy in task_copies:
        copy.start()
    exchange_ghosts(0)
    bend(0, 0, cells)
    for copy in task_copies:
        copy.wait()
    read_tasks()
    collect_ghosts(0)
    bend(0, cells, owners)
    run_tasks(0)
    drain_ghosts(0)

    own_slice[...] += velocities()
    move_out[...] = own_slice[...]

    def move_copy(o):
        return pltpu.make_async_remote_copy(
            src_ref=move_out,
            dst_ref=move_in.at[pl.ds(pl.multiple_of(cells * lane, 8), cells), :],
            send_sem=send_c.at[o],
            recv_sem=recv_c.at[lane],
            device_id=(space, 2 * lax.rem(plane + o, planes) + core),
            device_id_type=MESH,
        )

    def move_pass(o, which):
        origin = 2 * lax.rem(plane + planes - o, planes) + which
        at = pl.ds(pl.multiple_of(cells * origin, 8), cells)
        return pltpu.make_async_remote_copy(
            src_ref=move_out if o == 0 else move_in.at[at, :],
            dst_ref=move_in.at[at, :],
            send_sem=relay_c.at[o],
            recv_sem=recv_c.at[origin],
            device_id=(space, partner),
            device_id_type=MESH,
        )

    near_first = sorted(range(1, planes), key=lambda o: min(o, planes - o))
    for o in near_first:
        move_copy(o).start()
    move_pass(0, core).start()
    move_in[pl.ds(pl.multiple_of(cells * lane, 8), cells), :] = own_slice[...]
    spread_targets()
    for o in near_first:
        move_pass(o, core).wait_recv()
        move_pass(o, core).start()
    for o in range(planes):
        move_pass(o, 1 - core).wait_recv()
    whole = assemble([move_in[cells * n : cells * (n + 1), :] for n in range(lanes)], cells)
    for c in range(3):
        for k in range(chunks):
            at = c * pool_cells
            pool[1, at : at + cells, k * ROW : (k + 1) * ROW] = whole[c][k]

    stage_ghosts(1)
    exchange_ghosts(1)
    bend(1, 0, cells)
    for o in near_first:
        move_copy(o).wait_send()
    for o in range(planes):
        move_pass(o, core).wait_send()
    collect_ghosts(1)
    bend(1, cells, owners)
    run_tasks(1)
    drain_ghosts(1)

    speed = velocities()
    last_out[...] = jnp.zeros_like(last_out)
    for n in range(lanes):
        last_out[8 * n : 8 * n + share, :] = speed[n * share : (n + 1) * share, :]
    last_copies = lane_copies(
        lambda other: last_out.at[pl.ds(pl.multiple_of(8 * other, 8), 8), :],
        last_in,
        8,
        send_d,
        recv_d,
    )
    for copy in last_copies:
        copy.start()
    here = pl.ds(pl.multiple_of(8 * lane, 8), 8)
    last_in[here, :] = last_out[here, :]
    for copy in last_copies:
        copy.wait()
    whole = assemble([last_in[8 * n : 8 * (n + 1), :] for n in range(lanes)], 8)
    for c in range(3):
        speeds = jnp.concatenate(whole[c], axis=1)
        for n in range(share):
            cell = pool[1, pl.ds(c * pool_cells + share * lane + n, 1), :]
            vel_ref[c, n : n + 1, :] = speeds[n : n + 1, 0:points]
            moved_ref[c, n : n + 1, :] = (0.5 * (cell + speeds[n : n + 1, :]))[:, 0:points]


def shards(owners, lanes, positions, bend_op, send_list, task_target, task_source, task_count):
    cells, _, points = positions.shape
    cap = task_target.shape[1]
    slots = cap + 7 * (lanes - 1)
    width = -(-points // ROW) * ROW
    chunks = width // ROW
    piece = points // lanes
    rows_piece = -(-piece // 8) * 8
    cell_rows = 3 * rows_piece
    box_rows = -(-3 * chunks // 8) * 8
    share = cells // lanes
    pool_cells = cells + owners
    half = owners // 2
    planes = lanes // 2
    f32 = jnp.float32
    vmem = pl.BlockSpec(memory_space=pltpu.VMEM)
    hbm = pl.BlockSpec(memory_space=pltpu.HBM)
    dma = pltpu.SemaphoreType.DMA
    out = jax.ShapeDtypeStruct((3, share, points), f32)
    moved, velocity = pl.pallas_call(
        functools.partial(kernel, (owners, lanes, cells, points, cap, slots)),
        out_shape=(out, out),
        in_specs=[hbm] * 6,
        out_specs=(vmem, vmem),
        scratch_shapes=[
            pltpu.VMEM((ITERS, 3 * pool_cells, width), f32),
            pltpu.VMEM((3 * pool_cells, width), f32),
            pltpu.VMEM((width, width), jnp.bfloat16),
            pltpu.VMEM((width, width), jnp.bfloat16),
            pltpu.VMEM((ITERS, half * box_rows, ROW), f32),
            pltpu.VMEM((ITERS, owners * box_rows, ROW), f32),
            pltpu.VMEM((cells, cell_rows + 24, ROW), f32),
            pltpu.VMEM((ROW, ROW), f32),
            pltpu.VMEM((cells, ROW), f32),
            pltpu.VMEM((cells, ROW), f32),
            pltpu.VMEM((lanes * cells, ROW), f32),
            pltpu.VMEM((lanes * 8, ROW), f32),
            pltpu.VMEM((lanes * 8, ROW), f32),
            pltpu.VMEM((8, ROW), jnp.int32),
            pltpu.VMEM((lanes * 8, ROW), jnp.int32),
            pltpu.VMEM((8, ROW), jnp.int32),
            pltpu.SMEM((8, ROW), jnp.int32),
            dma((ITERS, half)),
            dma((ITERS, owners)),
            dma((ITERS, half)),
            dma((planes,)),
            dma((lanes,)),
            dma((planes,)),
            dma((lanes,)),
            dma((lanes,)),
            dma((lanes,)),
            dma((lanes,)),
            dma,
            pltpu.VMEM((3, cells, points), f32),
            pltpu.VMEM(bend_op.shape, f32),
            pltpu.SMEM(send_list.shape, jnp.int32),
            pltpu.VMEM((1, cap), jnp.int32),
            pltpu.VMEM((1, cap), jnp.int32),
            pltpu.VMEM((1, 1), jnp.int32),
            dma((6,)),
            pltpu.VMEM((24, ROW), f32),
        ],
        compiler_params=pltpu.CompilerParams(
            collective_id=0, has_side_effects=True, vmem_limit_bytes=67_043_328
        ),
    )(
        jnp.transpose(positions, (1, 0, 2)),
        bend_op,
        send_list,
        task_target,
        task_source,
        task_count.reshape(1, 1),
    )
    return jnp.transpose(moved, (1, 0, 2)), jnp.transpose(velocity, (1, 0, 2))


def solution(mesh):
    owners, lanes = mesh.shape["space"], mesh.shape["lane"]
    in_specs = (
        P("space", None, None),
        P(),
        P("space", None),
        P(("space", "lane"), None),
        P(("space", "lane"), None),
        P(("space", "lane")),
    )
    out_specs = (P(("space", "lane"), None, None), P(("space", "lane"), None, None))
    return jax.shard_map(
        functools.partial(shards, owners, lanes),
        mesh=mesh,
        in_specs=in_specs,
        out_specs=out_specs,
        check_vma=False,
    )
```
